128 devices in a mesh: gx: 16 (over x, y), gy: 8 (over z, core).
Axes of the slice: x: 4, y: 4, z: 4, core: 2. Of those that a mesh axis runs over, the one named last changes fastest.
Arguments:
- height_start: float32 [32, 2048, 1024], P(None, 'gx', 'gy'), may hold values from -6 to 6
- flow_x_start: float32 [32, 2048, 1024], P(None, 'gx', 'gy'), may hold values from -6 to 6
- flow_y_start: float32 [32, 2048, 1024], P(None, 'gx', 'gy'), may hold values from -6 to 6
- depth_field: float32 [2048, 1024], P('gx', 'gy'), may hold values from 0.2 to 1.2
- misfit_rows: float32 [32768, 128], P(('gx', 'gy')), may hold values from -6 to 6
- tile_list: int32 [32768, 1], P(('gx', 'gy')), may hold values from 0 to 127; in each aligned block of 256 rows (0 to 255, 256 to 511, ...) at most 4 rows name the same one
- member_list: int32 [32768], P(('gx', 'gy')), may hold values from 0 to 31
- cell_list: int32 [32768], P(('gx', 'gy')), may hold values from 0 to 16383
- count_list: int32 [32768], P(('gx', 'gy')), may hold values from 1 to 128
Outputs:
- height_adjoint: float32 [32, 2048, 1024], P(None, 'gx', 'gy')
- flow_x_adjoint: float32 [32, 2048, 1024], P(None, 'gx', 'gy')
- flow_y_adjoint: float32 [32, 2048, 1024], P(None, 'gx', 'gy')
The draws below stay inside these ranges and needn't reach their ends.
Inputs may be any that keep to these rules, and one draw needn't show every extreme that they name: `tile_list`: among the records of one device no tile is named more than 4 times.
All inputs are finite; a program needn't handle non-finite values.
Results may differ from the reference program's by a relative error of at most 0.00002.
Values sent between devices are 32-bit elements; how exact they have to be, the bound alone decides.
A program may use at most 128 MiB of HBM per device.

```python
import math
import jax
import jax.numpy as jnp
import numpy as np
from jax import lax

ENS = 32
TX = 128
TY = 128
REC_DEV = 256
SAMPLES = 128
STEPS = 32
CAP = 4
NX = 2048
NY = 1024
RECORDS = 32768
N_GY = 8
DEVICES = 128


def set_ends(values, rng, smallest, top_value):
    index_at = [jax.random.randint(jax.random.fold_in(rng, axis), (), 0, length) for axis, length in enumerate(values.shape)]
    widest = values.shape.index(max(values.shape))
    next_to = index_at[:widest] + [(index_at[widest] + 1) % values.shape[widest]] + index_at[widest + 1:]
    return values.at[tuple(index_at)].set(smallest).at[tuple(next_to)].set(top_value)


def levels(stream_key, shape, pieces, low, high):
    def one(dim, parts):
        heights = jax.random.uniform(jax.random.fold_in(jax.random.fold_in(stream_key, 6), dim), (parts,), jnp.float32, low / len(pieces), high / len(pieces))
        return jnp.repeat(jnp.exp(heights), shape[dim] // parts).reshape((-1,) + (1,) * (len(shape) - dim - 1))

    gain = one(*pieces[0])
    for cut in pieces[1:]:
        gain = gain * one(*cut)
    return gain


def shared_out(key, own, number, rows, number_of, top, bound, skew):
    sequence = jax.random.permutation(key, number_of)
    crowded, common = shares(number_of, rows * top, bound, skew, True), shares(number_of, rows * top, bound, skew, False)
    places = jnp.arange(number_of)

    def named(sizes, offset_by):
        used = int((sizes > 0).sum())
        fixed = max(1, used // 4)
        moved = fixed + (places - fixed + offset_by * (used - fixed)) % max(1, number_of - fixed)
        return jnp.zeros((number_of,), jnp.int32).at[sequence[jnp.where(places < fixed, places, moved)]].set(jnp.asarray(sizes, jnp.int32))

    sizes = jnp.where(number % 4 == 0, named(crowded, number // 4), named(common, number - number // 4 - 1))
    mixed = jax.random.permutation(jax.random.fold_in(own, 3), number_of)
    source_of, sink = mixed[0:number_of // 2 * 2:2], mixed[1:number_of // 2 * 2:2]
    room = jnp.minimum(sizes[source_of] - 1, bound - sizes[sink]) // 2
    room = jnp.where((source_of == sequence[0]) | (sink == sequence[0]) | (sizes[sink] == 0), 0, jnp.maximum(room, 0))
    moved = jax.random.randint(jax.random.fold_in(own, 4), (number_of // 2,), 0, 1 << 20) % (room + 1)
    sizes = sizes.at[source_of].add(-moved).at[sink].add(moved)
    labels = jnp.searchsorted(jnp.cumsum(sizes), jnp.arange(rows * top), side="right").astype(jnp.int32)
    listing = labels.reshape(top, rows).T
    listing = listing[jax.random.permutation(jax.random.fold_in(own, 1), rows)]
    offset_by = jax.random.randint(jax.random.fold_in(own, 2), (rows, 1), 0, top)
    return jnp.take_along_axis(listing, (jnp.arange(top)[None, :] + offset_by) % top, axis=1)


def shares(number_of, total, bound, skew, full):
    weights = [(1 << 20) // math.isqrt(grade ** skew) + 1 for grade in range(1, number_of + 1)]
    largest = bound if full else min(bound, max(-(-total // number_of), total * weights[0] // sum(weights)))
    least = 1 if total - largest >= number_of - 1 else 0
    given, surplus = [largest] + [least] * (number_of - 1), total - largest - least * (number_of - 1)
    while surplus > 0:
        movable = [i for i in range(1, number_of) if given[i] < largest] or [i for i in range(1, number_of) if given[i] < bound]
        mass, budget = sum([weights[i] for i in movable]), surplus
        for i in movable:
            more = min(bound - given[i], max(1, budget * weights[i] // mass), surplus)
            given[i] = given[i] + more
            surplus = surplus - more
    return np.array(given)


def gaussian(own_key, extent, scale, limit, split=(), kind=jnp.bfloat16):
    factor_of = levels(own_key, extent, split, -0.22, 0.18) if split else 1.0
    array = jax.random.normal(own_key, extent, jnp.float32) * scale * factor_of
    return jnp.minimum(jnp.maximum(array, -limit), limit).astype(kind)


def setup_inputs(seed: int = 0) -> dict:
    splits = jax.random.split(jax.random.key(seed), 10)
    height_start = gaussian(splits[0], (ENS, NX, NY), 1.0, 6.0, ((1, 16), (2, 8)), jnp.float32)
    flow_x_start = gaussian(splits[1], (ENS, NX, NY), 1.0, 6.0, ((1, 16), (2, 8)), jnp.float32)
    flow_y_start = gaussian(splits[2], (ENS, NX, NY), 1.0, 6.0, ((1, 16), (2, 8)), jnp.float32)
    depth_field = jnp.clip(jnp.exp(math.log(1.2) - 1.7917595 * jax.random.uniform(splits[3], (NX, NY), jnp.float32) ** levels(splits[3], (NX, NY), ((0, 16), (1, 8)), -0.2, 0.2)), 0.2, 1.2)
    misfit_rows = gaussian(splits[4], (RECORDS, SAMPLES), 1.0, 6.0, ((0, 128),), jnp.float32)
    tile_list_keys = jax.random.split(jax.random.fold_in(splits[5], 1), RECORDS // REC_DEV)
    tile_list_turns = jax.random.permutation(jax.random.fold_in(splits[5], 3), RECORDS // REC_DEV)
    tile_list = jax.vmap(lambda own, number: shared_out(jax.random.fold_in(splits[5], 2), own, number, REC_DEV, DEVICES, 1, CAP, 2))(tile_list_keys, tile_list_turns).reshape((RECORDS, 1))
    member_list = set_ends(jax.random.randint(splits[6], (RECORDS,), 0, ENS), jax.random.fold_in(splits[6], 1), 0, ENS - 1).astype(jnp.int32)
    cell_list = set_ends(jax.random.randint(splits[7], (RECORDS,), 0, TX * TY), jax.random.fold_in(splits[7], 1), 0, (TX * TY) - 1).astype(jnp.int32)
    count_list = set_ends(jax.random.randint(splits[8], (RECORDS,), 1, SAMPLES + 1), jax.random.fold_in(splits[8], 1), 1, SAMPLES).astype(jnp.int32)
    return {"height_start": height_start, "flow_x_start": flow_x_start, "flow_y_start": flow_y_start, "depth_field": depth_field, "misfit_rows": misfit_rows, "tile_list": tile_list, "member_list": member_list, "cell_list": cell_list, "count_list": count_list}


def reference(height_start, flow_x_start, flow_y_start, depth_field, misfit_rows, tile_list, member_list, cell_list, count_list):
    width = SAMPLES // STEPS
    sample_pos = jnp.arange(SAMPLES, dtype=jnp.int32)
    live = sample_pos[None, :] < count_list[:, None]
    masked = jnp.where(live, misfit_rows, jnp.zeros_like(misfit_rows))
    increments = jnp.sum(masked.reshape(-1, STEPS, width), axis=2)
    tiles = tile_list[:, 0]
    grid_row = (tiles // N_GY) * TX + cell_list // TY
    grid_col = (tiles % N_GY) * TY + cell_list % TY
    flat_index = ((member_list * NX + grid_row) * NY + grid_col).astype(jnp.int32)
    depth = depth_field[None, :, :]

    def advance(step, state):
        height, flow_x, flow_y = state
        amounts = lax.dynamic_index_in_dim(increments, step, 1, keepdims=False)
        height = height.reshape(-1).at[flat_index].add(amounts).reshape(height.shape)
        zero_row = jnp.zeros((height.shape[0], 1, height.shape[2]), height.dtype)
        zero_col = jnp.zeros((height.shape[0], height.shape[1], 1), height.dtype)
        next_x = jnp.concatenate([height[:, 1:, :], zero_row], axis=1)
        next_y = jnp.concatenate([height[:, :, 1:], zero_col], axis=2)
        flow_x = flow_x - 0.6 * (next_x - height)
        flow_y = flow_y - 0.6 * (next_y - height)
        flux_x = depth * flow_x
        flux_y = depth * flow_y
        prev_x = jnp.concatenate([zero_row, flux_x[:, :-1, :]], axis=1)
        prev_y = jnp.concatenate([zero_col, flux_y[:, :, :-1]], axis=2)
        height = height - 0.6 * ((flux_x - prev_x) + (flux_y - prev_y))
        return (height, flow_x, flow_y)

    height, flow_x, flow_y = lax.fori_loop(0, STEPS, advance, (height_start, flow_x_start, flow_y_start))
    return (height, flow_x, flow_y)
```

```python
import jax
import jax.numpy as jnp
from jax import lax
from jax.experimental import pallas as pl
from jax.experimental.pallas import tpu as pltpu
from jax.sharding import PartitionSpec as P

MESH = pl.DeviceIdType.MESH
F32 = jnp.float32
BF16 = jnp.bfloat16
STEPS = 32
EVENTS = 32
TILE = 128
GROUPS = 4
XI = 32
YI = 16
PY = YI + 1
SLOTS = 4
CELLS = TILE * TILE * EVENTS // 128


def three(x):
    high = x.astype(BF16)
    rest = x - high.astype(F32)
    mid = rest.astype(BF16)
    low = (rest - mid.astype(F32)).astype(BF16)
    return high, mid, low


def dot(a, b):
    return jnp.dot(a, b, preferred_element_type=F32)


def iota(shape, axis):
    return lax.broadcasted_iota(jnp.int32, shape, axis)


def slot_kernel(rows_ref, meta_ref, out_ref):
    records = rows_ref.shape[0]
    tile, member, cell, count = (meta_ref[i : i + 1, :] for i in range(4))
    hit = tile == iota((128, records), 0)
    earlier_mask = jnp.where(iota((records, records), 0) < iota((records, records), 1), 1.0, 0.0)
    rank = dot(jnp.where(hit, 1.0, 0.0).astype(BF16), earlier_mask.astype(BF16)).astype(jnp.int32)
    x, y = cell // TILE, cell % TILE
    vector_row = ((x % XI) * TILE + (y % YI) * 8 + y // YI).astype(F32)
    lane_of = ((x // XI) * EVENTS + member).astype(F32)
    countf = count.astype(F32)
    parts = three(rows_ref[...])
    lane = iota((128, 128), 1)
    total = jnp.zeros((128, 128), F32)
    ids = jnp.full((128, 128), -1.0, F32)
    for j in range(SLOTS):
        sel = hit & (rank == j)
        pick = jnp.where(sel, 1.0, 0.0).astype(BF16)
        found = dot(pick, parts[0]) + dot(pick, parts[1]) + dot(pick, parts[2])

        def of(value):
            return jnp.sum(jnp.where(sel, value, 0.0), axis=1, keepdims=True)

        found = jnp.where(lane.astype(F32) < of(countf), found, 0.0)
        window = jnp.where(iota((128, 128), 0) // 4 + STEPS * j == lane, 1.0, 0.0).astype(BF16)
        a, b, c = three(found)
        total = total + (dot(a, window) + dot(b, window) + dot(c, window))
        ids = jnp.where(lane == j, of(vector_row + 1.0) - 1.0, ids)
        ids = jnp.where(lane == SLOTS + j, of(lane_of + 1.0) - 1.0, ids)
    out_ref[:, 0:128] = total
    out_ref[:, 128:256] = ids


def sweep_kernel(
    p_in, q_in, r_in, depth_ref, slots_ref, p_out, q_out, r_out,
    stage, p2, wf, vf, cf, inj, onehot, rhs, lanes_of, inc,
    send_buf, recv_buf, init_send, init_recv, wh, ch, vh, chy,
    in_sem, out_sem, send_sem, recv_sem, init_send_sem, init_recv_sem,
):
    gx, gy = lax.axis_index("gx"), lax.axis_index("gy")
    nx, ny = lax.axis_size("gx"), lax.axis_size("gy")
    target = [(gx + 1, gy), (gx - 1, gy), (gx, gy + 1), (gx, gy - 1)]
    sends = [gx < nx - 1, gx > 0, gy < ny - 1, gy > 0]
    receives = [sends[1], sends[0], sends[3], sends[2]]

    loads = [
        pltpu.make_async_copy(src, stage.at[i], in_sem.at[i])
        for i, src in enumerate((p_in, q_in, r_in))
    ]
    for copy in loads:
        copy.start()
    recv_buf[...] = jnp.zeros_like(recv_buf)
    init_recv[...] = jnp.zeros_like(init_recv)

    barrier = pltpu.get_barrier_semaphore()
    for d in range(4):

        @pl.when(sends[d])
        def _():
            pl.semaphore_signal(barrier, inc=1, device_id=target[d], device_id_type=MESH)

    pl.semaphore_wait(barrier, sum(jnp.where(peer, 1, 0) for peer in sends))

    def edge_copy(d, slot):
        return pltpu.make_async_remote_copy(
            src_ref=send_buf.at[d, slot],
            dst_ref=recv_buf.at[d, slot],
            send_sem=send_sem.at[d, slot],
            recv_sem=recv_sem.at[d, slot],
            device_id=target[d],
            device_id_type=MESH,
        )

    def init_copy(i):
        return pltpu.make_async_remote_copy(
            src_ref=init_send.at[i],
            dst_ref=init_recv.at[i],
            send_sem=init_send_sem.at[i],
            recv_sem=init_recv_sem.at[i],
            device_id=target[2 * i],
            device_id_type=MESH,
        )

    lane = iota((8, 128), 1)
    sub = iota((8, 128), 0)
    group = lane // EVENTS

    def tile(ref, row):
        return ref[pl.ds(pl.multiple_of(row, 8), 8), :]

    def put(ref, row, value):
        ref[pl.ds(pl.multiple_of(row, 8), 8), :] = value

    def p_row(x, y):
        return (x * PY + y) * 8

    def w_row(x, y):
        return ((x + 1) * YI + y) * 8

    def v_row(x, y):
        return (x * PY + y + 1) * 8

    def c_row(x, y):
        return (x * YI + y) * 8

    def pack_x(load, source):
        packed = []
        for j in range(4):
            total = None
            for g in range(GROUPS):
                value = load(4 * j + g)
                shift = ((g - source) * EVENTS) % 128
                if shift:
                    value = pltpu.roll(value, shift, axis=1)
                total = value if total is None else jnp.where(group == g, value, total)
            packed.append(total)
        return packed

    def unpack_x(ref, y, to):
        value = ref[pl.ds((y // 4) * 8, 8), :]
        shift = ((to - y % 4) * EVENTS) % 128
        return pltpu.roll(value, shift, axis=1) if shift else value

    inc[...] = slots_ref[:, 0:128]
    ids = slots_ref[:, 128:256]
    rows_of = ids.T
    for j in range(SLOTS):
        lanes_of[pl.ds(j * 128, 128), :] = jnp.broadcast_to(ids[:, SLOTS + j : SLOTS + j + 1], (128, 128))

    def fill_onehot(i, carry):
        first = i * 128
        row = (iota((128, 128), 0) + first).astype(F32)
        for j in range(SLOTS):
            match = jnp.where(row == rows_of[j : j + 1, :], 1.0, 0.0)
            onehot[pl.ds(pl.multiple_of(first, 128), 128), pl.ds(j * 128, 128)] = match.astype(BF16)
        return carry

    lax.fori_loop(0, CELLS // 128, fill_onehot, 0)

    def inject(dst):
        lanes = iota((128, 128), 1).astype(F32)
        for j in range(SLOTS):
            column = inc[:, j * STEPS : j * STEPS + 1]
            value = jnp.where(lanes_of[pl.ds(j * 128, 128), :] == lanes, column, 0.0)
            for i, part in enumerate(three(value)):
                rhs[pl.ds(j * 128, 128), pl.ds(i * 128, 128)] = part
        inc[...] = pltpu.roll(inc[...], 127, axis=1)

        def chunk(i, carry):
            first = pl.multiple_of(i * 512, 512)
            out = dot(onehot[pl.ds(first, 512), :], rhs[...])
            dst[pl.ds(first, 512), :] = (out[:, 0:128] + out[:, 128:256]) + out[:, 256:384]
            return carry

        lax.fori_loop(0, CELLS // 512, chunk, 0)

    inject(inj.at[0])
    inject(inj.at[1])

    for copy in loads:
        copy.wait()
    p0 = p2.at[0]

    def bring(x, carry):
        def turned(ref):
            parts = [ref[pl.ds(g * XI + x, EVENTS, stride=TILE), :] for g in range(GROUPS)]
            return jnp.concatenate(parts, axis=0).T

        def spread(ref, base, value):
            for g in range(8):
                ref[pl.ds(base + g, YI, stride=8), :] = value[g * YI : (g + 1) * YI, :]

        deep = jnp.concatenate(
            [jnp.broadcast_to(depth_ref[pl.ds(g * XI + x, 1), :], (EVENTS, TILE)) for g in range(GROUPS)],
            axis=0,
        ).T
        scaled = deep * 0.6
        spread(cf, c_row(x, 0), scaled * 0.6)
        spread(p0, p_row(x, 0), turned(stage.at[0]))
        spread(wf, w_row(x, 0), turned(stage.at[1]) * scaled)
        spread(vf, v_row(x, 0), turned(stage.at[2]) * scaled)
        for y in range(YI):
            put(p0, p_row(x, y), tile(p0, p_row(x, y)) + tile(inj.at[0], c_row(x, y)))
        return carry

    lax.fori_loop(0, XI, bring, 0)

    def send_edges(ref, slot):
        def pack(d):
            if d == 0:
                value = jnp.concatenate(pack_x(lambda y: tile(ref, p_row(XI - 1, y)), GROUPS - 1), axis=0)
            elif d == 1:
                value = jnp.concatenate(pack_x(lambda y: tile(ref, p_row(0, y)), 0), axis=0)
            elif d == 2:
                value = ref[pl.ds((YI - 1) * 8 + 7, XI, stride=PY * 8), :]
            else:
                value = ref[pl.ds(0, XI, stride=PY * 8), :]
            send_buf[d, slot] = value

        for d in range(4):
            pack(d)

            @pl.when(sends[d])
            def _():
                edge_copy(d, slot).start()

    send_edges(p0, 0)
    init_send[0, 0:32] = jnp.concatenate(pack_x(lambda y: tile(wf, w_row(XI - 1, y)), GROUPS - 1), axis=0)
    init_send[0, 32:64] = jnp.concatenate(pack_x(lambda y: tile(cf, c_row(XI - 1, y)), GROUPS - 1), axis=0)
    init_send[1, 0:32] = vf[pl.ds(v_row(0, YI - 1) + 7, XI, stride=PY * 8), :]
    init_send[1, 32:64] = cf[pl.ds(c_row(0, YI - 1) + 7, XI, stride=YI * 8), :]
    for i in range(2):

        @pl.when(sends[2 * i])
        def _():
            init_copy(i).start()

    for i in range(2):

        @pl.when(receives[2 * i])
        def _():
            init_copy(i).wait_recv()

    for y in range(YI):
        wh[pl.ds(y * 8, 8), :] = jnp.where(group == 0, unpack_x(init_recv.at[0, pl.ds(0, 32)], y, 0), 0.0)
        ch[pl.ds(y * 8, 8), :] = jnp.where(group == 0, unpack_x(init_recv.at[0, pl.ds(32, 32)], y, 0), 0.0)
    vh[...] = init_recv[1, 0:32]
    chy[...] = init_recv[1, 32:64]

    def step(now, later, last):
        pc, pn = p2.at[now], p2.at[later]
        add = None if last else inj.at[later]
        for d in range(4):

            @pl.when(receives[d])
            def _():
                edge_copy(d, now).wait_recv()

        for y in range(YI):
            own = tile(pc, p_row(0, y))
            beyond = unpack_x(recv_buf.at[1, now], y, GROUPS - 1)
            put(pc, p_row(XI, y), jnp.where(lane < 128 - EVENTS, pltpu.roll(own, 128 - EVENTS, axis=1), beyond))
            before = unpack_x(recv_buf.at[0, now], y, 0)
            rows = pl.ds(y * 8, 8)
            wh[rows, :] = wh[rows, :] - ch[rows, :] * (own - before)
        vh[...] = vh[...] - chy[...] * (pc[pl.ds(0, XI, stride=PY * 8), :] - recv_buf[2, now])
        for x in range(XI):
            beyond = jnp.broadcast_to(recv_buf[3, now, pl.ds(x, 1), :], (8, 128))
            put(pc, p_row(x, YI), jnp.where(sub < 7, pltpu.roll(tile(pc, p_row(x, 0)), 7, axis=0), beyond))

        def flow(x, columns):
            for y in columns:
                own, c = tile(pc, p_row(x, y)), tile(cf, c_row(x, y))
                put(wf, w_row(x, y), tile(wf, w_row(x, y)) - c * (tile(pc, p_row(x + 1, y)) - own))
                put(vf, v_row(x, y), tile(vf, v_row(x, y)) - c * (tile(pc, p_row(x, y + 1)) - own))

        def height(x, columns):
            for y in columns:
                out = tile(pc, p_row(x, y)) - (
                    (tile(wf, w_row(x, y)) - tile(wf, w_row(x - 1, y)))
                    + (tile(vf, v_row(x, y)) - tile(vf, v_row(x, y - 1)))
                )
                if add is not None:
                    out = out + tile(add, c_row(x, y))
                put(pn, p_row(x, y), out)

        def over(first, end, body):
            lax.fori_loop(first, end, lambda x, carry: (body(x), carry)[1], 0)

        everywhere = range(YI)
        for x in (0, XI - 2, XI - 1):
            flow(x, everywhere)
        over(1, XI - 2, lambda x: flow(x, (0, YI - 2, YI - 1)))
        for y in range(YI):
            own = tile(wf, w_row(XI - 1, y))
            put(wf, w_row(-1, y), jnp.where(group > 0, pltpu.roll(own, EVENTS, axis=1), wh[pl.ds(y * 8, 8), :]))
        for x in range(XI):
            before = jnp.broadcast_to(vh[pl.ds(x, 1), :], (8, 128))
            own = tile(vf, v_row(x, YI - 1))
            put(vf, v_row(x, -1), jnp.where(sub > 0, pltpu.roll(own, 1, axis=0), before))
        for x in (0, XI - 1):
            height(x, everywhere)
        over(1, XI - 1, lambda x: height(x, (0, YI - 1)))
        if not last:
            for d in range(4):

                @pl.when(sends[d])
                def _():
                    edge_copy(d, now).wait_send()

            send_edges(pn, later)

        def inside(x):
            flow(x, range(1, YI - 2))
            height(x, range(1, YI - 1))

        over(1, XI - 2, inside)
        height(XI - 2, range(1, YI - 1))
        if last:
            for d in range(4):

                @pl.when(sends[d])
                def _():
                    edge_copy(d, now).wait_send()

    def advance(t, carry):
        now = lax.rem(t, 2)
        step(now, 1 - now, False)
        inject(inj.at[now])
        return carry

    lax.fori_loop(0, STEPS - 1, advance, 0)
    step((STEPS - 1) % 2, STEPS % 2, True)
    for i in range(2):

        @pl.when(sends[2 * i])
        def _():
            init_copy(i).wait_send()

    stores = []
    final = p2.at[STEPS % 2]
    for i, (ref, row, out) in enumerate(((final, p_row, p_out), (wf, w_row, q_out), (vf, v_row, r_out))):

        def back(x, carry, i=i, ref=ref, row=row):
            def gathered(source, base):
                parts = [source[pl.ds(base + g, YI, stride=8), :] for g in range(8)]
                return jnp.concatenate(parts, axis=0)

            value = gathered(ref, row(x, 0))
            if i:
                value = value * (0.6 / gathered(cf, c_row(x, 0)))
            turned = value.T
            for g in range(GROUPS):
                stage[i, pl.ds(g * XI + x, EVENTS, stride=TILE), :] = turned[g * EVENTS : (g + 1) * EVENTS, :]
            return carry

        lax.fori_loop(0, XI, back, 0)
        copy = pltpu.make_async_copy(stage.at[i], out, out_sem.at[i])
        copy.start()
        stores.append(copy)
    for copy in stores:
        copy.wait()


def local(
    height_start, flow_x_start, flow_y_start, depth_field,
    misfit_rows, tile_list, member_list, cell_list, count_list,
):
    shape = height_start.shape
    meta = jnp.stack([tile_list[:, 0], member_list, cell_list, count_list])
    vmem = pl.BlockSpec(memory_space=pltpu.VMEM)
    hbm = pl.BlockSpec(memory_space=pl.ANY)
    slots = pl.pallas_call(
        slot_kernel,
        out_shape=jax.ShapeDtypeStruct((128, 256), F32),
        in_specs=[vmem, vmem],
        out_specs=vmem,
    )(misfit_rows, meta)
    slots = lax.all_to_all(slots, ("gx", "gy"), split_axis=0, concat_axis=0, tiled=True)
    field = jax.ShapeDtypeStruct((CELLS, 128), F32)
    flat = [a.reshape(CELLS, 128) for a in (height_start, flow_x_start, flow_y_start)]
    outs = pl.pallas_call(
        sweep_kernel,
        out_shape=(field, field, field),
        in_specs=[hbm, hbm, hbm, vmem, vmem],
        out_specs=(hbm, hbm, hbm),
        scratch_shapes=[
            pltpu.VMEM((3, CELLS, 128), F32),
            pltpu.VMEM((2, (XI + 1) * PY * 8, 128), F32),
            pltpu.VMEM(((XI + 1) * YI * 8, 128), F32),
            pltpu.VMEM((XI * PY * 8, 128), F32),
            pltpu.VMEM((CELLS, 128), F32),
            pltpu.VMEM((2, CELLS, 128), F32),
            pltpu.VMEM((CELLS, SLOTS * 128), BF16),
            pltpu.VMEM((SLOTS * 128, 3 * 128), BF16),
            pltpu.VMEM((SLOTS * 128, 128), F32),
            pltpu.VMEM((128, 128), F32),
            pltpu.VMEM((4, 2, 32, 128), F32),
            pltpu.VMEM((4, 2, 32, 128), F32),
            pltpu.VMEM((2, 64, 128), F32),
            pltpu.VMEM((2, 64, 128), F32),
            pltpu.VMEM((128, 128), F32),
            pltpu.VMEM((128, 128), F32),
            pltpu.VMEM((32, 128), F32),
            pltpu.VMEM((32, 128), F32),
            pltpu.SemaphoreType.DMA((3,)),
            pltpu.SemaphoreType.DMA((3,)),
            pltpu.SemaphoreType.DMA((4, 2)),
            pltpu.SemaphoreType.DMA((4, 2)),
            pltpu.SemaphoreType.DMA((2,)),
            pltpu.SemaphoreType.DMA((2,)),
        ],
        compiler_params=pltpu.CompilerParams(
            collective_id=0, has_side_effects=True, vmem_limit_bytes=48 * 1024 * 1024
        ),
    )(*flat, depth_field, slots)
    return tuple(a.reshape(shape) for a in outs)


def solution(mesh):
    in_specs = (
        P(None, "gx", "gy"),
        P(None, "gx", "gy"),
        P(None, "gx", "gy"),
        P("gx", "gy"),
        P(("gx", "gy"), None),
        P(("gx", "gy"), None),
        P(("gx", "gy")),
        P(("gx", "gy")),
        P(("gx", "gy")),
    )
    out_specs = (P(None, "gx", "gy"), P(None, "gx", "gy"), P(None, "gx", "gy"))
    return jax.shard_map(local, mesh=mesh, in_specs=in_specs, out_specs=out_specs, check_vma=False)
```

```python
import jax
import jax.numpy as jnp
from jax import lax
from jax.experimental import pallas as pl
from jax.experimental.pallas import tpu as pltpu
from jax.sharding import PartitionSpec as P

MESH = pl.DeviceIdType.MESH
F32 = jnp.float32
BF16 = jnp.bfloat16
STEPS = 32
EVENTS = 32
TILE = 128
GROUPS = 4
XI = 32
YI = 16
PY = YI + 1
SLOTS = 4
CELLS = TILE * TILE * EVENTS // 128
TILES = CELLS // 8
TURNS = XI - 3
SHARE = 9
PLACES = 640
EMPTY = 2 * TURNS * SHARE
MIDDLE = EMPTY + 1


def three(x):
    high = x.astype(BF16)
    rest = x - high.astype(F32)
    mid = rest.astype(BF16)
    low = (rest - mid.astype(F32)).astype(BF16)
    return high, mid, low


def dot(a, b):
    return jnp.dot(a, b, preferred_element_type=F32)


def iota(shape, axis):
    return lax.broadcasted_iota(jnp.int32, shape, axis)


def slot_kernel(rows_ref, meta_ref, out_ref):
    records = rows_ref.shape[0]
    tile, member, cell, count = (meta_ref[i : i + 1, :] for i in range(4))
    hit = tile == iota((128, records), 0)
    earlier_mask = jnp.where(iota((records, records), 0) < iota((records, records), 1), 1.0, 0.0)
    rank = dot(jnp.where(hit, 1.0, 0.0).astype(BF16), earlier_mask.astype(BF16)).astype(jnp.int32)
    x, y = cell // TILE, cell % TILE
    vector_row = ((x % XI) * TILE + (y % YI) * 8 + y // YI).astype(F32)
    lane_of = ((x // XI) * EVENTS + member).astype(F32)
    countf = count.astype(F32)
    parts = three(rows_ref[...])
    lane = iota((128, 128), 1)
    total = jnp.zeros((128, 128), F32)
    ids = jnp.full((128, 128), -1.0, F32)
    for j in range(SLOTS):
        sel = hit & (rank == j)
        pick = jnp.where(sel, 1.0, 0.0).astype(BF16)
        found = dot(pick, parts[0]) + dot(pick, parts[1]) + dot(pick, parts[2])

        def of(value):
            return jnp.sum(jnp.where(sel, value, 0.0), axis=1, keepdims=True)

        found = jnp.where(lane.astype(F32) < of(countf), found, 0.0)
        window = jnp.where(iota((128, 128), 0) // 4 + STEPS * j == lane, 1.0, 0.0).astype(BF16)
        a, b, c = three(found)
        total = total + (dot(a, window) + dot(b, window) + dot(c, window))
        ids = jnp.where(lane == j, of(vector_row + 1.0) - 1.0, ids)
        ids = jnp.where(lane == SLOTS + j, of(lane_of + 1.0) - 1.0, ids)
    out_ref[:, 0:128] = total
    out_ref[:, 128:256] = ids


def prep_kernel(slots_ref, values_ref, keep_ref, place_ref, last_ref):
    slots = SLOTS * 128
    half = slots // 2
    ids = slots_ref[:, 128:256]
    turned = ids.T
    rows = jnp.concatenate([ids[:, j : j + 1] for j in range(SLOTS)], axis=0).astype(jnp.int32)
    lanes = jnp.concatenate([ids[:, SLOTS + j : SLOTS + j + 1] for j in range(SLOTS)], axis=0).astype(jnp.int32)
    across = jnp.concatenate([turned[j : j + 1, :] for j in range(SLOTS)], axis=1).astype(jnp.int32)
    down_tile = jnp.where(rows < 0, TILES, rows >> 3)
    across_tile = jnp.where(across < 0, TILES, across >> 3)
    down_key = down_tile * slots + iota((slots, 1), 0)
    across_key = across_tile * slots + iota((1, slots), 1)

    def position(rank):
        upper = rank >= half
        away = jnp.where(upper, slots - 1 - rank, rank)
        turn = (away * 7282) >> 16
        return turn * (2 * SHARE) + (away - turn * SHARE) + jnp.where(upper, SHARE, 0)

    below = jnp.where(down_key < across_key, 1.0, 0.0)
    rank = jnp.sum(below, axis=0, keepdims=True).astype(jnp.int32)
    order = jnp.where(position(rank) == iota((PLACES, slots), 0), 1.0, 0.0).astype(BF16)
    above = jnp.sum(below, axis=1, keepdims=True)
    same = down_tile == across_tile
    same_above = jnp.sum(jnp.where(same, below, 0.0), axis=1, keepdims=True)
    same_below = jnp.sum(jnp.where(same, 1.0 - below, 0.0), axis=1, keepdims=True) - 1.0
    in_upper = above < half
    first_of = jnp.where(in_upper, same_above, same_below) < 0.5
    lane = iota((slots, 128), 1)
    increments = jnp.concatenate(
        [slots_ref[:, 0:128]] + [pltpu.roll(slots_ref[:, 0:128], 128 - STEPS * j, axis=1) for j in range(1, SLOTS)],
        axis=0,
    )
    table = jnp.where(lane < STEPS, increments, 0.0)
    table = jnp.where(lane == STEPS, ((rows & 7) * 128 + lanes).astype(F32), table)
    table = jnp.where(lane == STEPS + 1, jnp.where(first_of, 1.0, 0.0), table)
    a, b, c = three(table)
    ordered = (dot(order, a) + dot(order, b)) + dot(order, c)
    flat = ordered.T
    values_ref[...] = flat[0:STEPS, :]
    place_ref[...] = flat[STEPS : STEPS + 1, :].astype(jnp.int32)
    keep_ref[...] = 1.0 - flat[STEPS + 1 : STEPS + 2, :]
    wanted = iota((1, TILES), 1)
    upto = jnp.sum(jnp.where(down_tile <= wanted, 1.0, 0.0), axis=0, keepdims=True).astype(jnp.int32)
    before = jnp.sum(jnp.where(down_tile < wanted, 1.0, 0.0), axis=0, keepdims=True).astype(jnp.int32)
    last = upto - 1
    where = jnp.where(last < half, position(last), jnp.where(before >= half, position(before), MIDDLE))
    last_ref[...] = jnp.where(upto > before, where, EMPTY)


def sweep_kernel(
    p_in, q_in, r_in, depth_ref, values, keeps, places, lasts, p_out, q_out, r_out,
    stage, pa, pb, wf, vf, cf, ta, tb,
    send_buf, recv_buf, init_send, init_recv, wh, ch, vh, chy,
    in_sem, out_sem, send_sem, recv_sem, init_send_sem, init_recv_sem,
):
    gx, gy = lax.axis_index("gx"), lax.axis_index("gy")
    nx, ny = lax.axis_size("gx"), lax.axis_size("gy")
    target = [(gx + 1, gy), (gx - 1, gy), (gx, gy + 1), (gx, gy - 1)]
    sends = [gx < nx - 1, gx > 0, gy < ny - 1, gy > 0]
    receives = [sends[1], sends[0], sends[3], sends[2]]

    loads = [
        pltpu.make_async_copy(src, stage.at[i], in_sem.at[i])
        for i, src in enumerate((p_in, q_in, r_in))
    ]
    for copy in loads:
        copy.start()
    recv_buf[...] = jnp.zeros_like(recv_buf)
    init_recv[...] = jnp.zeros_like(init_recv)

    barrier = pltpu.get_barrier_semaphore()
    for d in range(4):

        @pl.when(sends[d])
        def _():
            pl.semaphore_signal(barrier, inc=1, device_id=target[d], device_id_type=MESH)

    pl.semaphore_wait(barrier, sum(jnp.where(peer, 1, 0) for peer in sends))

    def edge_copy(d, slot):
        return pltpu.make_async_remote_copy(
            src_ref=send_buf.at[d, slot],
            dst_ref=recv_buf.at[d, slot],
            send_sem=send_sem.at[d, slot],
            recv_sem=recv_sem.at[d, slot],
            device_id=target[d],
            device_id_type=MESH,
        )

    def init_copy(i):
        return pltpu.make_async_remote_copy(
            src_ref=init_send.at[i],
            dst_ref=init_recv.at[i],
            send_sem=init_send_sem.at[i],
            recv_sem=init_recv_sem.at[i],
            device_id=target[2 * i],
            device_id_type=MESH,
        )

    lane = iota((8, 128), 1)
    sub = iota((8, 128), 0)
    group = lane // EVENTS

    def tile(ref, row):
        return ref[pl.ds(pl.multiple_of(row, 8), 8), :]

    def put(ref, row, value):
        ref[pl.ds(pl.multiple_of(row, 8), 8), :] = value

    def p_row(x, y):
        return (x * PY + y) * 8

    def w_row(x, y):
        return ((x + 1) * YI + y) * 8

    def v_row(x, y):
        return (x * PY + y + 1) * 8

    def c_row(x, y):
        return (x * YI + y) * 8

    def pack_x(load, source):
        packed = []
        for j in range(4):
            total = None
            for g in range(GROUPS):
                value = load(4 * j + g)
                shift = ((g - source) * EVENTS) % 128
                if shift:
                    value = pltpu.roll(value, shift, axis=1)
                total = value if total is None else jnp.where(group == g, value, total)
            packed.append(total)
        return packed

    def unpack_x(ref, y, to):
        value = ref[pl.ds((y // 4) * 8, 8), :]
        shift = ((to - y % 4) * EVENTS) % 128
        return pltpu.roll(value, shift, axis=1) if shift else value

    place_iota = sub * 128 + lane

    def gathered(table, x, y):
        return table[lasts[x * YI + y]]

    def build(table, t, turn, carry):
        first, base = turn * (2 * SHARE), t * PLACES + turn * (2 * SHARE)
        carry = list(carry)
        for i in range(SHARE):
            for side in range(2):
                n = side * SHARE + i
                value = jnp.where(place_iota == places[first + n], values[base + n], 0.0)
                carry[side] = value + carry[side] * keeps[first + n]
                table[first + n] = carry[side]
        return tuple(carry)

    zero = jnp.zeros((8, 128), F32)
    for t, table in ((0, ta), (1, tb)):
        table[EMPTY] = zero
        ends = lax.fori_loop(0, TURNS, lambda i, carry: build(table, t, i, carry), (zero, zero))
        table[MIDDLE] = ends[0] + ends[1]

    for copy in loads:
        copy.wait()

    def bring(x, carry):
        def turned(ref):
            parts = [ref[pl.ds(g * XI + x, EVENTS, stride=TILE), :] for g in range(GROUPS)]
            return jnp.concatenate(parts, axis=0).T

        def spread(ref, base, value):
            for g in range(8):
                ref[pl.ds(base + g, YI, stride=8), :] = value[g * YI : (g + 1) * YI, :]

        deep = jnp.concatenate(
            [jnp.broadcast_to(depth_ref[pl.ds(g * XI + x, 1), :], (EVENTS, TILE)) for g in range(GROUPS)],
            axis=0,
        ).T
        scaled = deep * 0.6
        spread(cf, c_row(x, 0), scaled * 0.6)
        spread(pa, p_row(x, 0), turned(stage.at[0]))
        spread(wf, w_row(x, 0), turned(stage.at[1]) * scaled)
        spread(vf, v_row(x, 0), turned(stage.at[2]) * scaled)
        for y in range(YI):
            put(pa, p_row(x, y), tile(pa, p_row(x, y)) + gathered(ta, x, y))
        return carry

    lax.fori_loop(0, XI, bring, 0)

    def send_edges(ref, slot):
        def pack(d):
            if d == 0:
                value = jnp.concatenate(pack_x(lambda y: tile(ref, p_row(XI - 1, y)), GROUPS - 1), axis=0)
            elif d == 1:
                value = jnp.concatenate(pack_x(lambda y: tile(ref, p_row(0, y)), 0), axis=0)
            elif d == 2:
                value = ref[pl.ds((YI - 1) * 8 + 7, XI, stride=PY * 8), :]
            else:
                value = ref[pl.ds(0, XI, stride=PY * 8), :]
            send_buf[d, slot] = value

        for d in range(4):
            pack(d)

            @pl.when(sends[d])
            def _():
                edge_copy(d, slot).start()

    send_edges(pa, 0)
    init_send[0, 0:32] = jnp.concatenate(pack_x(lambda y: tile(wf, w_row(XI - 1, y)), GROUPS - 1), axis=0)
    init_send[0, 32:64] = jnp.concatenate(pack_x(lambda y: tile(cf, c_row(XI - 1, y)), GROUPS - 1), axis=0)
    init_send[1, 0:32] = vf[pl.ds(v_row(0, YI - 1) + 7, XI, stride=PY * 8), :]
    init_send[1, 32:64] = cf[pl.ds(c_row(0, YI - 1) + 7, XI, stride=YI * 8), :]
    for i in range(2):

        @pl.when(sends[2 * i])
        def _():
            init_copy(i).start()

    for i in range(2):

        @pl.when(receives[2 * i])
        def _():
            init_copy(i).wait_recv()

    for y in range(YI):
        wh[pl.ds(y * 8, 8), :] = jnp.where(group == 0, unpack_x(init_recv.at[0, pl.ds(0, 32)], y, 0), 0.0)
        ch[pl.ds(y * 8, 8), :] = jnp.where(group == 0, unpack_x(init_recv.at[0, pl.ds(32, 32)], y, 0), 0.0)
    vh[...] = init_recv[1, 0:32]
    chy[...] = init_recv[1, 32:64]

    def step(t, slot, pc, pn, table, build_table):
        def flow(x, y, own, right, down):
            c = tile(cf, c_row(x, y))
            w = tile(wf, w_row(x, y)) - c * (down - own)
            v = tile(vf, v_row(x, y)) - c * (right - own)
            put(wf, w_row(x, y), w)
            put(vf, v_row(x, y), v)
            return w, v

        def flow_row(x, columns):
            own = tile(pc, p_row(x, columns[0]))
            for y in columns:
                right = tile(pc, p_row(x, y + 1))
                flow(x, y, own, right, tile(pc, p_row(x + 1, y)))
                own = right

        def flow_column(first, count, y):
            own = tile(pc, p_row(first, y))
            for i in range(count):
                down = tile(pc, p_row(first + i + 1, y))
                flow(first + i, y, own, tile(pc, p_row(first + i, y + 1)), down)
                own = down

        def height(x, y, own, w, before, v, left):
            out = own - ((w - before) + (v - left))
            if table is not None:
                out = out + gathered(table, x, y)
            put(pn, p_row(x, y), out)

        def height_row(x, columns):
            left = tile(vf, v_row(x, columns[0] - 1))
            for y in columns:
                v = tile(vf, v_row(x, y))
                height(x, y, tile(pc, p_row(x, y)), tile(wf, w_row(x, y)), tile(wf, w_row(x - 1, y)), v, left)
                left = v

        def height_column(first, count, y):
            before = tile(wf, w_row(first - 1, y))
            for i in range(count):
                x = first + i
                w = tile(wf, w_row(x, y))
                height(x, y, tile(pc, p_row(x, y)), w, before, tile(vf, v_row(x, y)), tile(vf, v_row(x, y - 1)))
                before = w

        def turns(first, size, count, body):
            lax.fori_loop(0, count, lambda i, carry: (body(first + i * size), carry)[1], 0)

        for x in (0, XI - 2):
            flow_row(x, range(0, YI - 1))

        def before_columns(first, count=7):
            flow_column(first, count, 0)
            flow_column(first, count, YI - 2)

        turns(1, 7, 4, before_columns)
        before_columns(XI - 3, 1)

        for d in range(4):

            @pl.when(receives[d])
            def _():
                edge_copy(d, slot).wait_recv()

        for y in range(YI):
            own = tile(pc, p_row(0, y))
            beyond = unpack_x(recv_buf.at[1, slot], y, GROUPS - 1)
            put(pc, p_row(XI, y), jnp.where(lane < 128 - EVENTS, pltpu.roll(own, 128 - EVENTS, axis=1), beyond))
            before = unpack_x(recv_buf.at[0, slot], y, 0)
            rows = pl.ds(y * 8, 8)
            wh[rows, :] = wh[rows, :] - ch[rows, :] * (own - before)
        vh[...] = vh[...] - chy[...] * (pc[pl.ds(0, XI, stride=PY * 8), :] - recv_buf[2, slot])
        for x in range(XI):
            beyond = jnp.broadcast_to(recv_buf[3, slot, pl.ds(x, 1), :], (8, 128))
            put(pc, p_row(x, YI), jnp.where(sub < 7, pltpu.roll(tile(pc, p_row(x, 0)), 7, axis=0), beyond))

        flow_row(XI - 1, range(YI))
        flow_column(0, XI - 1, YI - 1)
        for y in range(YI):
            own = tile(wf, w_row(XI - 1, y))
            put(wf, w_row(-1, y), jnp.where(group > 0, pltpu.roll(own, EVENTS, axis=1), wh[pl.ds(y * 8, 8), :]))
        for x in range(XI):
            before = jnp.broadcast_to(vh[pl.ds(x, 1), :], (8, 128))
            own = tile(vf, v_row(x, YI - 1))
            put(vf, v_row(x, -1), jnp.where(sub > 0, pltpu.roll(own, 1, axis=0), before))
        for x in (0, XI - 1):
            height_row(x, range(YI))

        def edge_columns(first):
            height_column(first, 6, 0)
            height_column(first, 6, YI - 1)

        turns(1, 6, 5, edge_columns)
        for d in range(4):

            @pl.when(sends[d])
            def _():
                edge_copy(d, slot).wait_send()

        if table is not None:
            send_edges(pn, 1 - slot)

        def inside(i, carry):
            x = i + 1
            if build_table is not None:
                carry = build(build_table, t + 2, i, carry)
            own = tile(pc, p_row(x, 1))
            left = tile(vf, v_row(x, 0))
            for y in range(1, YI - 1):
                if y < YI - 2:
                    right = tile(pc, p_row(x, y + 1))
                    w, v = flow(x, y, own, right, tile(pc, p_row(x + 1, y)))
                else:
                    right = None
                    w, v = tile(wf, w_row(x, y)), tile(vf, v_row(x, y))
                height(x, y, own, w, tile(wf, w_row(x - 1, y)), v, left)
                own, left = right, v
            return carry

        ends = lax.fori_loop(0, TURNS, inside, (zero, zero))
        if build_table is not None:
            build_table[MIDDLE] = ends[0] + ends[1]
        height_row(XI - 2, range(1, YI - 1))

    def advance(i, carry):
        step(2 * i, 0, pa, pb, tb, ta)
        step(2 * i + 1, 1, pb, pa, ta, tb)
        return carry

    lax.fori_loop(0, STEPS // 2 - 1, advance, 0)
    step(STEPS - 2, 0, pa, pb, tb, None)
    step(STEPS - 1, 1, pb, pa, None, None)
    for i in range(2):

        @pl.when(sends[2 * i])
        def _():
            init_copy(i).wait_send()

    stores = []
    for i, (ref, row, out) in enumerate(((pa, p_row, p_out), (wf, w_row, q_out), (vf, v_row, r_out))):

        def back(x, carry, i=i, ref=ref, row=row):
            def collected(source, base):
                parts = [source[pl.ds(base + g, YI, stride=8), :] for g in range(8)]
                return jnp.concatenate(parts, axis=0)

            value = collected(ref, row(x, 0))
            if i:
                value = value * (0.6 / collected(cf, c_row(x, 0)))
            turned = value.T
            for g in range(GROUPS):
                stage[i, pl.ds(g * XI + x, EVENTS, stride=TILE), :] = turned[g * EVENTS : (g + 1) * EVENTS, :]
            return carry

        lax.fori_loop(0, XI, back, 0)
        copy = pltpu.make_async_copy(stage.at[i], out, out_sem.at[i])
        copy.start()
        stores.append(copy)
    for copy in stores:
        copy.wait()


def local(
    height_start, flow_x_start, flow_y_start, depth_field,
    misfit_rows, tile_list, member_list, cell_list, count_list,
):
    shape = height_start.shape
    meta = jnp.stack([tile_list[:, 0], member_list, cell_list, count_list])
    vmem = pl.BlockSpec(memory_space=pltpu.VMEM)
    hbm = pl.BlockSpec(memory_space=pl.ANY)
    slots = pl.pallas_call(
        slot_kernel,
        out_shape=jax.ShapeDtypeStruct((128, 256), F32),
        in_specs=[vmem, vmem],
        out_specs=vmem,
    )(misfit_rows, meta)
    slots = lax.all_to_all(slots, ("gx", "gy"), split_axis=0, concat_axis=0, tiled=True)
    tables = pl.pallas_call(
        prep_kernel,
        out_shape=(
            jax.ShapeDtypeStruct((STEPS, PLACES), F32),
            jax.ShapeDtypeStruct((1, PLACES), F32),
            jax.ShapeDtypeStruct((1, PLACES), jnp.int32),
            jax.ShapeDtypeStruct((1, TILES), jnp.int32),
        ),
        in_specs=[vmem],
        out_specs=(vmem,) * 4,
    )(slots)
    field = jax.ShapeDtypeStruct((CELLS, 128), F32)
    smem = pl.BlockSpec(memory_space=pltpu.SMEM)
    flat = [a.reshape(CELLS, 128) for a in (height_start, flow_x_start, flow_y_start)]
    outs = pl.pallas_call(
        sweep_kernel,
        out_shape=(field, field, field),
        in_specs=[hbm, hbm, hbm, vmem, smem, smem, smem, smem],
        out_specs=(hbm, hbm, hbm),
        scratch_shapes=[
            pltpu.VMEM((3, CELLS, 128), F32),
            pltpu.VMEM(((XI + 1) * PY * 8, 128), F32),
            pltpu.VMEM(((XI + 1) * PY * 8, 128), F32),
            pltpu.VMEM(((XI + 1) * YI * 8, 128), F32),
            pltpu.VMEM((XI * PY * 8, 128), F32),
            pltpu.VMEM((CELLS, 128), F32),
            pltpu.VMEM((MIDDLE + 1, 8, 128), F32),
            pltpu.VMEM((MIDDLE + 1, 8, 128), F32),
            pltpu.VMEM((4, 2, 32, 128), F32),
            pltpu.VMEM((4, 2, 32, 128), F32),
            pltpu.VMEM((2, 64, 128), F32),
            pltpu.VMEM((2, 64, 128), F32),
            pltpu.VMEM((128, 128), F32),
            pltpu.VMEM((128, 128), F32),
            pltpu.VMEM((32, 128), F32),
            pltpu.VMEM((32, 128), F32),
            pltpu.SemaphoreType.DMA((3,)),
            pltpu.SemaphoreType.DMA((3,)),
            pltpu.SemaphoreType.DMA((4, 2)),
            pltpu.SemaphoreType.DMA((4, 2)),
            pltpu.SemaphoreType.DMA((2,)),
            pltpu.SemaphoreType.DMA((2,)),
        ],
        compiler_params=pltpu.CompilerParams(
            collective_id=0, has_side_effects=True, vmem_limit_bytes=48 * 1024 * 1024
        ),
    )(*flat, depth_field, *(a.reshape(-1) for a in tables))
    return tuple(a.reshape(shape) for a in outs)


def solution(mesh):
    in_specs = (
        P(None, "gx", "gy"),
        P(None, "gx", "gy"),
        P(None, "gx", "gy"),
        P("gx", "gy"),
        P(("gx", "gy"), None),
        P(("gx", "gy"), None),
        P(("gx", "gy")),
        P(("gx", "gy")),
        P(("gx", "gy")),
    )
    out_specs = (P(None, "gx", "gy"), P(None, "gx", "gy"), P(None, "gx", "gy"))
    return jax.shard_map(local, mesh=mesh, in_specs=in_specs, out_specs=out_specs, check_vma=False)
```

```python
import jax
import jax.numpy as jnp
from jax import lax
from jax.experimental import pallas as pl
from jax.experimental.pallas import tpu as pltpu
from jax.sharding import PartitionSpec as P

MESH = pl.DeviceIdType.MESH
F32 = jnp.float32
BF16 = jnp.bfloat16
STEPS = 32
EVENTS = 32
TILE = 128
GROUPS = 4
XI = 32
YI = 16
PY = YI + 1
SLOTS = 4
CELLS = TILE * TILE * EVENTS // 128
TILES = CELLS // 8
TURNS = XI - 3
SHARE = 9
PLACES = 640
EMPTY = 2 * TURNS * SHARE
MIDDLE = EMPTY + 1


def three(x):
    high = x.astype(BF16)
    rest = x - high.astype(F32)
    mid = rest.astype(BF16)
    low = (rest - mid.astype(F32)).astype(BF16)
    return high, mid, low


def dot(a, b):
    return jnp.dot(a, b, preferred_element_type=F32)


def iota(shape, axis):
    return lax.broadcasted_iota(jnp.int32, shape, axis)


def slot_kernel(rows_ref, meta_ref, out_ref):
    records = rows_ref.shape[0]
    tile, member, cell, count = (meta_ref[i : i + 1, :] for i in range(4))
    hit = tile == iota((128, records), 0)
    earlier_mask = jnp.where(iota((records, records), 0) < iota((records, records), 1), 1.0, 0.0)
    rank = dot(jnp.where(hit, 1.0, 0.0).astype(BF16), earlier_mask.astype(BF16)).astype(jnp.int32)
    x, y = cell // TILE, cell % TILE
    vector_row = ((x % XI) * TILE + (y % YI) * 8 + y // YI).astype(F32)
    lane_of = ((x // XI) * EVENTS + member).astype(F32)
    countf = count.astype(F32)
    parts = three(rows_ref[...])
    lane = iota((128, 128), 1)
    total = jnp.zeros((128, 128), F32)
    ids = jnp.full((128, 128), -1.0, F32)
    for j in range(SLOTS):
        sel = hit & (rank == j)
        pick = jnp.where(sel, 1.0, 0.0).astype(BF16)
        found = dot(pick, parts[0]) + dot(pick, parts[1]) + dot(pick, parts[2])

        def of(value):
            return jnp.sum(jnp.where(sel, value, 0.0), axis=1, keepdims=True)

        found = jnp.where(lane.astype(F32) < of(countf), found, 0.0)
        window = jnp.where(iota((128, 128), 0) // 4 + STEPS * j == lane, 1.0, 0.0).astype(BF16)
        a, b, c = three(found)
        total = total + (dot(a, window) + dot(b, window) + dot(c, window))
        ids = jnp.where(lane == j, of(vector_row + 1.0) - 1.0, ids)
        ids = jnp.where(lane == SLOTS + j, of(lane_of + 1.0) - 1.0, ids)
    out_ref[:, 0:128] = total
    out_ref[:, 128:256] = ids


def prep_kernel(slots_ref, values_ref, keep_ref, place_ref, last_ref):
    slots = SLOTS * 128
    half = slots // 2
    ids = slots_ref[:, 128:256]
    turned = ids.T
    rows = jnp.concatenate([ids[:, j : j + 1] for j in range(SLOTS)], axis=0).astype(jnp.int32)
    lanes = jnp.concatenate([ids[:, SLOTS + j : SLOTS + j + 1] for j in range(SLOTS)], axis=0).astype(jnp.int32)
    across = jnp.concatenate([turned[j : j + 1, :] for j in range(SLOTS)], axis=1).astype(jnp.int32)
    down_tile = jnp.where(rows < 0, TILES, rows >> 3)
    across_tile = jnp.where(across < 0, TILES, across >> 3)
    down_key = down_tile * slots + iota((slots, 1), 0)
    across_key = across_tile * slots + iota((1, slots), 1)

    def position(rank):
        upper = rank >= half
        away = jnp.where(upper, slots - 1 - rank, rank)
        turn = (away * 7282) >> 16
        return turn * (2 * SHARE) + (away - turn * SHARE) + jnp.where(upper, SHARE, 0)

    below = jnp.where(down_key < across_key, 1.0, 0.0)
    rank = jnp.sum(below, axis=0, keepdims=True).astype(jnp.int32)
    order = jnp.where(position(rank) == iota((PLACES, slots), 0), 1.0, 0.0).astype(BF16)
    above = jnp.sum(below, axis=1, keepdims=True)
    same = down_tile == across_tile
    same_above = jnp.sum(jnp.where(same, below, 0.0), axis=1, keepdims=True)
    same_below = jnp.sum(jnp.where(same, 1.0 - below, 0.0), axis=1, keepdims=True) - 1.0
    in_upper = above < half
    first_of = jnp.where(in_upper, same_above, same_below) < 0.5
    lane = iota((slots, 128), 1)
    increments = jnp.concatenate(
        [slots_ref[:, 0:128]] + [pltpu.roll(slots_ref[:, 0:128], 128 - STEPS * j, axis=1) for j in range(1, SLOTS)],
        axis=0,
    )
    table = jnp.where(lane < STEPS, increments, 0.0)
    table = jnp.where(lane == STEPS, ((rows & 7) * 128 + lanes).astype(F32), table)
    table = jnp.where(lane == STEPS + 1, jnp.where(first_of, 1.0, 0.0), table)
    a, b, c = three(table)
    ordered = (dot(order, a) + dot(order, b)) + dot(order, c)
    flat = ordered.T
    values_ref[...] = flat[0:STEPS, :]
    place_ref[...] = flat[STEPS : STEPS + 1, :].astype(jnp.int32)
    keep_ref[...] = 1.0 - flat[STEPS + 1 : STEPS + 2, :]
    wanted = iota((1, TILES), 1)
    upto = jnp.sum(jnp.where(down_tile <= wanted, 1.0, 0.0), axis=0, keepdims=True).astype(jnp.int32)
    before = jnp.sum(jnp.where(down_tile < wanted, 1.0, 0.0), axis=0, keepdims=True).astype(jnp.int32)
    last = upto - 1
    where = jnp.where(last < half, position(last), jnp.where(before >= half, position(before), MIDDLE))
    last_ref[...] = jnp.where(upto > before, where, EMPTY)


def sweep_kernel(
    p_in, q_in, r_in, depth_ref, values, keeps, places, lasts, p_out, q_out, r_out,
    stage, pa, pb, wf, vf, cf, ta, tb,
    send_buf, recv_buf, init_send, init_recv, wh, ch, vh, chy,
    in_sem, out_sem, send_sem, recv_sem, init_send_sem, init_recv_sem,
):
    gx, gy = lax.axis_index("gx"), lax.axis_index("gy")
    nx, ny = lax.axis_size("gx"), lax.axis_size("gy")
    target = [(gx + 1, gy), (gx - 1, gy), (gx, gy + 1), (gx, gy - 1)]
    sends = [gx < nx - 1, gx > 0, gy < ny - 1, gy > 0]
    receives = [sends[1], sends[0], sends[3], sends[2]]

    loads = [
        pltpu.make_async_copy(src, stage.at[i], in_sem.at[i])
        for i, src in enumerate((p_in, q_in, r_in))
    ]
    for copy in loads:
        copy.start()
    recv_buf[...] = jnp.zeros_like(recv_buf)
    init_recv[...] = jnp.zeros_like(init_recv)

    barrier = pltpu.get_barrier_semaphore()
    for d in range(4):

        @pl.when(sends[d])
        def _():
            pl.semaphore_signal(barrier, inc=1, device_id=target[d], device_id_type=MESH)

    pl.semaphore_wait(barrier, sum(jnp.where(peer, 1, 0) for peer in sends))

    def edge_copy(d, slot):
        return pltpu.make_async_remote_copy(
            src_ref=send_buf.at[d, slot],
            dst_ref=recv_buf.at[d, slot],
            send_sem=send_sem.at[d, slot],
            recv_sem=recv_sem.at[d, slot],
            device_id=target[d],
            device_id_type=MESH,
        )

    def init_copy(i):
        return pltpu.make_async_remote_copy(
            src_ref=init_send.at[i],
            dst_ref=init_recv.at[i],
            send_sem=init_send_sem.at[i],
            recv_sem=init_recv_sem.at[i],
            device_id=target[2 * i],
            device_id_type=MESH,
        )

    lane = iota((8, 128), 1)
    sub = iota((8, 128), 0)
    group = lane // EVENTS

    def tile(ref, row):
        return ref[pl.ds(pl.multiple_of(row, 8), 8), :]

    def put(ref, row, value):
        ref[pl.ds(pl.multiple_of(row, 8), 8), :] = value

    def p_row(x, y):
        return (x * PY + y) * 8

    def w_row(x, y):
        return ((x + 1) * YI + y) * 8

    def v_row(x, y):
        return (x * PY + y + 1) * 8

    def c_row(x, y):
        return (x * YI + y) * 8

    def pack_x(load, source):
        packed = []
        for j in range(4):
            total = None
            for g in range(GROUPS):
                value = load(4 * j + g)
                shift = ((g - source) * EVENTS) % 128
                if shift:
                    value = pltpu.roll(value, shift, axis=1)
                total = value if total is None else jnp.where(group == g, value, total)
            packed.append(total)
        return packed

    def unpack_x(ref, y, to):
        value = ref[pl.ds((y // 4) * 8, 8), :]
        shift = ((to - y % 4) * EVENTS) % 128
        return pltpu.roll(value, shift, axis=1) if shift else value

    place_iota = sub * 128 + lane

    def gathered(table, x, y):
        return table[lasts[x * YI + y]]

    def build(table, t, turn, carry):
        first, base = turn * (2 * SHARE), t * PLACES + turn * (2 * SHARE)
        carry = list(carry)
        for i in range(SHARE):
            for side in range(2):
                n = side * SHARE + i
                value = jnp.where(place_iota == places[first + n], values[base + n], 0.0)
                carry[side] = value + carry[side] * keeps[first + n]
                table[first + n] = carry[side]
        return tuple(carry)

    zero = jnp.zeros((8, 128), F32)
    for t, table in ((0, ta), (1, tb)):
        table[EMPTY] = zero
        ends = lax.fori_loop(0, TURNS, lambda i, carry: build(table, t, i, carry), (zero, zero))
        table[MIDDLE] = ends[0] + ends[1]

    for copy in loads:
        copy.wait()

    def bring(x, carry):
        def turned(ref):
            parts = [ref[pl.ds(g * XI + x, EVENTS, stride=TILE), :] for g in range(GROUPS)]
            return jnp.concatenate(parts, axis=0).T

        def spread(ref, base, value):
            for g in range(8):
                ref[pl.ds(base + g, YI, stride=8), :] = value[g * YI : (g + 1) * YI, :]

        deep = jnp.concatenate(
            [jnp.broadcast_to(depth_ref[pl.ds(g * XI + x, 1), :], (EVENTS, TILE)) for g in range(GROUPS)],
            axis=0,
        ).T
        scaled = deep * 0.6
        spread(cf, c_row(x, 0), scaled * 0.6)
        spread(pa, p_row(x, 0), turned(stage.at[0]))
        spread(wf, w_row(x, 0), turned(stage.at[1]) * scaled)
        spread(vf, v_row(x, 0), turned(stage.at[2]) * scaled)
        for y in range(YI):
            put(pa, p_row(x, y), tile(pa, p_row(x, y)) + gathered(ta, x, y))
        return carry

    lax.fori_loop(0, XI, bring, 0)

    def send_edges(ref, slot):
        def pack(d):
            if d == 0:
                value = jnp.concatenate(pack_x(lambda y: tile(ref, p_row(XI - 1, y)), GROUPS - 1), axis=0)
            elif d == 1:
                value = jnp.concatenate(pack_x(lambda y: tile(ref, p_row(0, y)), 0), axis=0)
            elif d == 2:
                value = ref[pl.ds((YI - 1) * 8 + 7, XI, stride=PY * 8), :]
            else:
                value = ref[pl.ds(0, XI, stride=PY * 8), :]
            send_buf[d, slot] = value

        for d in range(4):
            pack(d)

            @pl.when(sends[d])
            def _():
                edge_copy(d, slot).start()

    send_edges(pa, 0)
    init_send[0, 0:32] = jnp.concatenate(pack_x(lambda y: tile(wf, w_row(XI - 1, y)), GROUPS - 1), axis=0)
    init_send[0, 32:64] = jnp.concatenate(pack_x(lambda y: tile(cf, c_row(XI - 1, y)), GROUPS - 1), axis=0)
    init_send[1, 0:32] = vf[pl.ds(v_row(0, YI - 1) + 7, XI, stride=PY * 8), :]
    init_send[1, 32:64] = cf[pl.ds(c_row(0, YI - 1) + 7, XI, stride=YI * 8), :]
    for i in range(2):

        @pl.when(sends[2 * i])
        def _():
            init_copy(i).start()

    for i in range(2):

        @pl.when(receives[2 * i])
        def _():
            init_copy(i).wait_recv()

    for y in range(YI):
        wh[pl.ds(y * 8, 8), :] = jnp.where(group == 0, unpack_x(init_recv.at[0, pl.ds(0, 32)], y, 0), 0.0)
        ch[pl.ds(y * 8, 8), :] = jnp.where(group == 0, unpack_x(init_recv.at[0, pl.ds(32, 32)], y, 0), 0.0)
    vh[...] = init_recv[1, 0:32]
    chy[...] = init_recv[1, 32:64]

    def step(t, slot, pc, pn, table, build_table):
        def flow(x, y, own, right, down):
            c = tile(cf, c_row(x, y))
            w = tile(wf, w_row(x, y)) - c * (down - own)
            v = tile(vf, v_row(x, y)) - c * (right - own)
            put(wf, w_row(x, y), w)
            put(vf, v_row(x, y), v)
            return w, v

        def flow_row(x, columns):
            own = tile(pc, p_row(x, columns[0]))
            for y in columns:
                right = tile(pc, p_row(x, y + 1))
                flow(x, y, own, right, tile(pc, p_row(x + 1, y)))
                own = right

        def flow_column(first, count, y):
            own = tile(pc, p_row(first, y))
            for i in range(count):
                down = tile(pc, p_row(first + i + 1, y))
                flow(first + i, y, own, tile(pc, p_row(first + i, y + 1)), down)
                own = down

        def height(x, y, own, w, before, v, left):
            out = own - ((w - before) + (v - left))
            if table is not None:
                out = out + gathered(table, x, y)
            put(pn, p_row(x, y), out)

        def height_row(x, columns):
            left = tile(vf, v_row(x, columns[0] - 1))
            for y in columns:
                v = tile(vf, v_row(x, y))
                height(x, y, tile(pc, p_row(x, y)), tile(wf, w_row(x, y)), tile(wf, w_row(x - 1, y)), v, left)
                left = v

        def height_column(first, count, y):
            before = tile(wf, w_row(first - 1, y))
            for i in range(count):
                x = first + i
                w = tile(wf, w_row(x, y))
                height(x, y, tile(pc, p_row(x, y)), w, before, tile(vf, v_row(x, y)), tile(vf, v_row(x, y - 1)))
                before = w

        def turns(first, size, count, body):
            lax.fori_loop(0, count, lambda i, carry: (body(first + i * size), carry)[1], 0)

        for x in (0, XI - 2):
            flow_row(x, range(0, YI - 1))

        def before_columns(first, count=7):
            flow_column(first, count, 0)
            flow_column(first, count, YI - 2)

        turns(1, 7, 4, before_columns)
        before_columns(XI - 3, 1)

        def arrive(directions):
            for d in directions:

                @pl.when(receives[d])
                def _():
                    edge_copy(d, slot).wait_recv()

        def beyond_left(x):
            before = jnp.broadcast_to(vh[pl.ds(x, 1), :], (8, 128))
            own = tile(vf, v_row(x, YI - 1))
            put(vf, v_row(x, -1), jnp.where(sub > 0, pltpu.roll(own, 1, axis=0), before))

        arrive((2, 3))
        vh[...] = vh[...] - chy[...] * (pc[pl.ds(0, XI, stride=PY * 8), :] - recv_buf[2, slot])
        for x in range(XI):
            beyond = jnp.broadcast_to(recv_buf[3, slot, pl.ds(x, 1), :], (8, 128))
            put(pc, p_row(x, YI), jnp.where(sub < 7, pltpu.roll(tile(pc, p_row(x, 0)), 7, axis=0), beyond))
        flow_column(0, XI - 1, YI - 1)
        for x in range(XI - 1):
            beyond_left(x)

        def edge_columns(first):
            height_column(first, 6, 0)
            height_column(first, 6, YI - 1)

        turns(1, 6, 5, edge_columns)

        arrive((0, 1))
        for y in range(YI):
            own = tile(pc, p_row(0, y))
            beyond = unpack_x(recv_buf.at[1, slot], y, GROUPS - 1)
            put(pc, p_row(XI, y), jnp.where(lane < 128 - EVENTS, pltpu.roll(own, 128 - EVENTS, axis=1), beyond))
            before = unpack_x(recv_buf.at[0, slot], y, 0)
            rows = pl.ds(y * 8, 8)
            wh[rows, :] = wh[rows, :] - ch[rows, :] * (own - before)
        flow_row(XI - 1, range(YI))
        for y in range(YI):
            own = tile(wf, w_row(XI - 1, y))
            put(wf, w_row(-1, y), jnp.where(group > 0, pltpu.roll(own, EVENTS, axis=1), wh[pl.ds(y * 8, 8), :]))
        beyond_left(XI - 1)
        for x in (0, XI - 1):
            height_row(x, range(YI))
        for d in range(4):

            @pl.when(sends[d])
            def _():
                edge_copy(d, slot).wait_send()

        if table is not None:
            send_edges(pn, 1 - slot)

        def inside(i, carry):
            x = i + 1
            if build_table is not None:
                carry = build(build_table, t + 2, i, carry)
            own = tile(pc, p_row(x, 1))
            left = tile(vf, v_row(x, 0))
            for y in range(1, YI - 1):
                if y < YI - 2:
                    right = tile(pc, p_row(x, y + 1))
                    w, v = flow(x, y, own, right, tile(pc, p_row(x + 1, y)))
                else:
                    right = None
                    w, v = tile(wf, w_row(x, y)), tile(vf, v_row(x, y))
                height(x, y, own, w, tile(wf, w_row(x - 1, y)), v, left)
                own, left = right, v
            return carry

        ends = lax.fori_loop(0, TURNS, inside, (zero, zero))
        if build_table is not None:
            build_table[MIDDLE] = ends[0] + ends[1]
        height_row(XI - 2, range(1, YI - 1))

    def advance(i, carry):
        step(2 * i, 0, pa, pb, tb, ta)
        step(2 * i + 1, 1, pb, pa, ta, tb)
        return carry

    lax.fori_loop(0, STEPS // 2 - 1, advance, 0)
    step(STEPS - 2, 0, pa, pb, tb, None)
    step(STEPS - 1, 1, pb, pa, None, None)
    for i in range(2):

        @pl.when(sends[2 * i])
        def _():
            init_copy(i).wait_send()

    stores = []
    for i, (ref, row, out) in enumerate(((pa, p_row, p_out), (wf, w_row, q_out), (vf, v_row, r_out))):

        def back(x, carry, i=i, ref=ref, row=row):
            def collected(source, base):
                parts = [source[pl.ds(base + g, YI, stride=8), :] for g in range(8)]
                return jnp.concatenate(parts, axis=0)

            value = collected(ref, row(x, 0))
            if i:
                value = value * (0.6 / collected(cf, c_row(x, 0)))
            turned = value.T
            for g in range(GROUPS):
                stage[i, pl.ds(g * XI + x, EVENTS, stride=TILE), :] = turned[g * EVENTS : (g + 1) * EVENTS, :]
            return carry

        lax.fori_loop(0, XI, back, 0)
        copy = pltpu.make_async_copy(stage.at[i], out, out_sem.at[i])
        copy.start()
        stores.append(copy)
    for copy in stores:
        copy.wait()


def local(
    height_start, flow_x_start, flow_y_start, depth_field,
    misfit_rows, tile_list, member_list, cell_list, count_list,
):
    shape = height_start.shape
    meta = jnp.stack([tile_list[:, 0], member_list, cell_list, count_list])
    vmem = pl.BlockSpec(memory_space=pltpu.VMEM)
    hbm = pl.BlockSpec(memory_space=pl.ANY)
    slots = pl.pallas_call(
        slot_kernel,
        out_shape=jax.ShapeDtypeStruct((128, 256), F32),
        in_specs=[vmem, vmem],
        out_specs=vmem,
    )(misfit_rows, meta)
    slots = lax.all_to_all(slots, ("gx", "gy"), split_axis=0, concat_axis=0, tiled=True)
    tables = pl.pallas_call(
        prep_kernel,
        out_shape=(
            jax.ShapeDtypeStruct((STEPS, PLACES), F32),
            jax.ShapeDtypeStruct((1, PLACES), F32),
            jax.ShapeDtypeStruct((1, PLACES), jnp.int32),
            jax.ShapeDtypeStruct((1, TILES), jnp.int32),
        ),
        in_specs=[vmem],
        out_specs=(vmem,) * 4,
    )(slots)
    field = jax.ShapeDtypeStruct((CELLS, 128), F32)
    smem = pl.BlockSpec(memory_space=pltpu.SMEM)
    flat = [a.reshape(CELLS, 128) for a in (height_start, flow_x_start, flow_y_start)]
    outs = pl.pallas_call(
        sweep_kernel,
        out_shape=(field, field, field),
        in_specs=[hbm, hbm, hbm, vmem, smem, smem, smem, smem],
        out_specs=(hbm, hbm, hbm),
        scratch_shapes=[
            pltpu.VMEM((3, CELLS, 128), F32),
            pltpu.VMEM(((XI + 1) * PY * 8, 128), F32),
            pltpu.VMEM(((XI + 1) * PY * 8, 128), F32),
            pltpu.VMEM(((XI + 1) * YI * 8, 128), F32),
            pltpu.VMEM((XI * PY * 8, 128), F32),
            pltpu.VMEM((CELLS, 128), F32),
            pltpu.VMEM((MIDDLE + 1, 8, 128), F32),
            pltpu.VMEM((MIDDLE + 1, 8, 128), F32),
            pltpu.VMEM((4, 2, 32, 128), F32),
            pltpu.VMEM((4, 2, 32, 128), F32),
            pltpu.VMEM((2, 64, 128), F32),
            pltpu.VMEM((2, 64, 128), F32),
            pltpu.VMEM((128, 128), F32),
            pltpu.VMEM((128, 128), F32),
            pltpu.VMEM((32, 128), F32),
            pltpu.VMEM((32, 128), F32),
            pltpu.SemaphoreType.DMA((3,)),
            pltpu.SemaphoreType.DMA((3,)),
            pltpu.SemaphoreType.DMA((4, 2)),
            pltpu.SemaphoreType.DMA((4, 2)),
            pltpu.SemaphoreType.DMA((2,)),
            pltpu.SemaphoreType.DMA((2,)),
        ],
        compiler_params=pltpu.CompilerParams(
            collective_id=0, has_side_effects=True, vmem_limit_bytes=48 * 1024 * 1024
        ),
    )(*flat, depth_field, *(a.reshape(-1) for a in tables))
    return tuple(a.reshape(shape) for a in outs)


def solution(mesh):
    in_specs = (
        P(None, "gx", "gy"),
        P(None, "gx", "gy"),
        P(None, "gx", "gy"),
        P("gx", "gy"),
        P(("gx", "gy"), None),
        P(("gx", "gy"), None),
        P(("gx", "gy")),
        P(("gx", "gy")),
        P(("gx", "gy")),
    )
    out_specs = (P(None, "gx", "gy"), P(None, "gx", "gy"), P(None, "gx", "gy"))
    return jax.shard_map(local, mesh=mesh, in_specs=in_specs, out_specs=out_specs, check_vma=False)
```
